32 devices in a mesh: py: 8 (over y, x, core), pz: 4 (over z).
Axes of the slice: x: 2, y: 2, z: 4, core: 2. Of those that a mesh axis runs over, the one named last changes fastest.
Arguments:
- velocity: float32 [3, 32, 128, 2048], P(None, ('py', 'pz')), may hold values from -6 to 6
- fluid: float32 [32, 128, 2048], P(('py', 'pz')), may hold values from 0.1 to 1
- pressure: float32 [32, 128, 2048], P(None, 'pz', 'py'), may hold values from -4 to 4
Outputs:
- projected: float32 [3, 32, 128, 2048], P(None, ('py', 'pz'))
- divergence: float32 [32, 128, 2048], P(None, 'pz', 'py')
The draws below stay inside these ranges and needn't reach their ends.
All inputs are finite; a program needn't handle non-finite values.
Results may differ from the reference program's by a relative error of at most 0.00002.
Values sent between devices are 32-bit elements; how exact they have to be, the bound alone decides.
A program may use at most 64 MiB of HBM per device.

```python
import jax
import jax.numpy as jnp
from jax import lax

NY = 2048
NZ = 128
NX = 32


def shard_levels(rng, shape, shards, low, high):
    loudness, own = 1.0, jax.random.fold_in(rng, 6)
    for dim, shards_of in shards:
        draws = jnp.exp(jax.random.uniform(jax.random.fold_in(own, dim), (shards_of,), jnp.float32, low / len(shards), high / len(shards)))
        loudness = loudness * jnp.repeat(draws, shape[dim] // shards_of).reshape([-1 if axis == dim else 1 for axis in range(len(shape))])
    return loudness


def bell_draw(key, shape, deviation, limit, cuts=(), held_as=jnp.bfloat16):
    array = jax.random.normal(key, shape, jnp.float32) * deviation
    if len(cuts) > 0:
        array = shard_levels(key, shape, cuts, -0.22, 0.18) * array
    return jnp.clip(array, min=-limit, max=limit).astype(held_as)


def setup_inputs(seed: int = 0) -> dict:
    splits = jax.random.split(jax.random.key(seed), 4)
    velocity = bell_draw(splits[0], (3, NX, NZ, NY), 1.0, 6.0, ((1, 32),), jnp.float32)
    fluid = jnp.clip(0.1 + 0.9 * jax.random.uniform(splits[1], (NX, NZ, NY), jnp.float32) ** shard_levels(splits[1], (NX, NZ, NY), ((0, 32),), -0.2, 0.2), 0.1, 1.0)
    pressure = bell_draw(splits[2], (NX, NZ, NY), 0.5, 4.0, ((1, 4), (2, 8)), jnp.float32)
    return {"velocity": velocity, "fluid": fluid, "pressure": pressure}


def face_update(component, fluid, pressure, axis):
    index = lax.broadcasted_iota(jnp.int32, fluid.shape, axis)
    fluid_prev = jnp.roll(fluid, 1, axis)
    pressure_prev = jnp.roll(pressure, 1, axis)
    weight = jnp.where(index == 0, jnp.float32(0.0), 0.5 * (fluid + fluid_prev))
    return weight * (component - (pressure - pressure_prev))


def forward_difference(updated, axis):
    index = lax.broadcasted_iota(jnp.int32, updated.shape, axis)
    following = jnp.where(index == updated.shape[axis] - 1, jnp.float32(0.0), jnp.roll(updated, -1, axis))
    return following - updated


def reference(velocity, fluid, pressure):
    parts = []
    divergence = jnp.zeros(fluid.shape, jnp.float32)
    for axis in range(3):
        updated = face_update(velocity[axis], fluid, pressure, axis)
        divergence = divergence + forward_difference(updated, axis)
        parts.append(updated)
    return jnp.stack(parts, 0), divergence
```

```python
import functools

import jax
import jax.numpy as jnp
from jax import lax
from jax.experimental import pallas as pl
from jax.experimental.pallas import tpu as pltpu
from jax.sharding import PartitionSpec as P

AHEAD = 2
LANES = 128


def kernel(
    count_y, count_z, v_hbm, f_hbm, p_hbm, out_hbm, div_hbm,
    v, f, f_low, main, halo, left, out, part, next_x, got, got_x, div,
    in_sem, put_sem,
    main_s, main_r, halo_s, halo_r, edge_s, edge_r, f_s, f_r, fwd_s, fwd_r, nx_s, nx_r,
    a_s, a_r, x_s, x_r,
):
    py = lax.axis_index("py")
    pz = lax.axis_index("pz")
    me = py * count_z + pz
    planes = count_y * count_z
    rows, across = f.shape
    width = across // count_y
    part_rows = rows // count_z
    half = count_z // 2 if count_z % 2 == 0 else 1
    half_rows = half * part_rows

    def side(z):
        return z // half if isinstance(z, int) else lax.div(z, half)

    def joined(z):
        return min((z + 1) % half, 1) if isinstance(z, int) else jnp.minimum(lax.rem(z + 1, half), 1)

    def cols(c):
        return pl.ds(pl.multiple_of(c * width, width), width)

    def band(g):
        return pl.ds(g * part_rows, part_rows)

    other = pl.ds(pl.multiple_of(jnp.where(side(pz) == 0, rows - half_rows, 0), part_rows), half_rows)

    def wrap(c):
        return lax.rem(c + 2 * count_y, count_y)

    def remote(src, dst, send, recv, y, z):
        return pltpu.make_async_remote_copy(
            src_ref=src, dst_ref=dst, send_sem=send, recv_sem=recv,
            device_id=(y, z), device_id_type=pl.DeviceIdType.MESH,
        )

    def begin(src, dst, send, recv, y, z, gate=1, away=False):
        apart = 1 if away else jnp.abs(y * count_z + z - me)

        @pl.when(jnp.minimum(gate, apart) > 0)
        def _():
            remote(src, dst, send, recv, y, z).start()

        if not away:
            @pl.when(gate - jnp.minimum(apart, 1) > 0)
            def _():
                pltpu.make_async_copy(src, dst, recv).start()

    def sent(src, dst, send, recv, y, z, gate=1, away=False):
        apart = 1 if away else jnp.abs(y * count_z + z - me)

        @pl.when(jnp.minimum(gate, apart) > 0)
        def _():
            remote(src, dst, send, recv, y, z).wait_send()

    def landed(dst, recv):
        pltpu.make_async_copy(dst, dst, recv).wait()

    def direct(z, g):
        return 1 - joined(z - 1) * jnp.minimum(jnp.abs(side(g) - side(z)), 1)

    loads = [
        pltpu.make_async_copy(v_hbm.at[:, 0], v, in_sem.at[0]),
        pltpu.make_async_copy(f_hbm.at[0], f, in_sem.at[1]),
    ]
    for load in loads:
        load.start()

    barrier = pltpu.get_barrier_semaphore()

    def greet(i, carry):
        @pl.when(i != me)
        def _():
            pl.semaphore_signal(
                barrier, inc=1, device_id=(lax.div(i, count_z), lax.rem(i, count_z)),
                device_id_type=pl.DeviceIdType.MESH,
            )
        return carry

    lax.fori_loop(0, planes, greet, 0)
    pl.semaphore_wait(barrier, planes - 1)

    mine = pl.ds(pl.multiple_of(pz * part_rows, part_rows), part_rows)
    ahead_y = lax.div(me + 1, count_z)
    ahead_z = lax.rem(me + 1, count_z)

    def pressure_sends(k, do):
        y = wrap(py - k)
        for z in range(count_z):
            target = y * count_z + z
            slot = k * count_z + z
            do(p_hbm.at[target], main.at[mine, cols(py)], main_s.at[slot], main_r.at[k * count_z + pz], y, z)

            do(p_hbm.at[jnp.maximum(target - 1, 0)], halo.at[mine, cols(py)],
               halo_s.at[slot], halo_r.at[k * count_z + pz], y, z, gate=direct(z, pz))
        c = cols(wrap(ahead_y + k))
        do(f_hbm.at[0, :, c], f_low.at[:, c], f_s.at[k], f_r.at[k], ahead_y, ahead_z,
           gate=planes - 1 - me, away=True)

    def edge_sends(do):
        for z in range(count_z):
            y = wrap(py + 1)
            do(p_hbm.at[y * count_z + z, :, width - LANES:], left.at[mine],
               edge_s.at[z], edge_r.at[pz], y, z, away=True)

    def forward(k, do):
        c = cols(wrap(py + k))
        do(main.at[other, c], halo.at[other, c], fwd_s.at[k], fwd_r.at[k], py, pz + 1,
           gate=joined(pz), away=True)

    def lend(k, do):
        c = cols(wrap(py + k))
        do(out.at[0, other, c], next_x.at[:, c], nx_s.at[k], nx_r.at[k], py, pz - 1,
           gate=joined(pz - 1), away=True)

    def result_sends(k, do):
        y = wrap(py + k)
        for z in range(count_z):
            slot = k * count_z + z
            do(part.at[band(z), cols(y)], got.at[me], a_s.at[slot], a_r.at[me], y, z)
            below = jnp.maximum(me - 1, 0)
            do(out.at[0, band(z), cols(y)], got_x.at[below], x_s.at[slot], x_r.at[below], y, z,
               gate=jnp.minimum(me, direct(pz, z)))

    edge_sends(begin)
    for k in range(min(AHEAD, count_y)):
        pressure_sends(k, begin)
    for load in loads:
        load.wait()
    for z in range(count_z):
        landed(left.at[band(z)], edge_r.at[z])

    def before(tile, values):
        wide = jnp.concatenate([tile, values], 1)
        return pltpu.roll(wide, 1, 1)[:, LANES:]

    def project(k):
        @pl.when(k + AHEAD < count_y)
        def _():
            pressure_sends(k + AHEAD, begin)

        y = wrap(py + k)
        c = cols(y)
        for z in range(count_z):
            landed(main.at[band(z), c], main_r.at[k * count_z + z])
        forward(k, begin)
        for z in range(count_z):
            @pl.when(direct(pz, z) > 0)
            def _():
                landed(halo.at[band(z), c], halo_r.at[k * count_z + z])

        @pl.when(joined(pz - 1) > 0)
        def _():
            landed(halo.at[other, c], fwd_r.at[k])

        @pl.when(me > 0)
        def _():
            landed(f_low.at[:, c], f_r.at[k])

        fluid = f[:, c]
        here = main[:, c]
        w_x = 0.5 * (fluid + f_low[:, c])
        along_x = w_x * (v[0, :, c] - (here - halo[:, c]))
        out[0, :, c] = jnp.where(me == 0, jnp.float32(0.0), along_x)
        lend(k, begin)
        z_index = lax.broadcasted_iota(jnp.int32, fluid.shape, 0)
        w_z = 0.5 * (fluid + pltpu.roll(fluid, 1, 0))
        along_z = w_z * (v[1, :, c] - (here - pltpu.roll(here, 1, 0)))
        out[1, :, c] = jnp.where(z_index == 0, jnp.float32(0.0), along_z)
        y_index = lax.broadcasted_iota(jnp.int32, fluid.shape, 1) + y * width
        f_tile = f[:, pl.ds(pl.multiple_of(wrap(y - 1) * width + (width - LANES), LANES), LANES)]
        w_y = 0.5 * (fluid + before(f_tile, fluid))
        along_y = w_y * (v[2, :, c] - (here - before(left[...], here)))
        out[2, :, c] = jnp.where(y_index == 0, jnp.float32(0.0), along_y)
        left[...] = here[:, width - LANES:]
        pltpu.make_async_copy(out.at[:, :, c], out_hbm.at[:, 0, :, c], put_sem.at[k]).start()

    def diverge(k):
        y = wrap(py + k)
        c = cols(y)
        along_z = out[1, :, c]
        along_y = out[2, :, c]
        z_index = lax.broadcasted_iota(jnp.int32, along_z.shape, 0)
        y_index = lax.broadcasted_iota(jnp.int32, along_z.shape, 1) + y * width
        z_next = jnp.where(z_index == rows - 1, jnp.float32(0.0), pltpu.roll(along_z, rows - 1, 0))
        tile = out[2, :, pl.ds(pl.multiple_of(wrap(y + 1) * width, width), LANES)]
        wide = pltpu.roll(jnp.concatenate([along_y, tile], 1), width + LANES - 1, 1)[:, :width]
        y_next = jnp.where(y_index == across - 1, jnp.float32(0.0), wide)
        part[:, c] = (z_next - along_z) + (y_next - along_y) - out[0, :, c]

        @pl.when(joined(pz) > 0)
        def _():
            landed(next_x.at[:, c], nx_r.at[k])
            part[other, c] = part[other, c] + next_x[:, c]

        result_sends(k, begin)

    def step(k, carry):
        @pl.when(k < count_y)
        def _():
            project(k)

        @pl.when(k > 0)
        def _():
            diverge(k - 1)
        return carry

    lax.fori_loop(0, count_y + 1, step, 0)

    def collect(i, carry):
        y = wrap(py - i - 1)
        for z in range(count_z):
            q = y * count_z + z
            landed(got.at[q], a_r.at[q])
            added = jnp.minimum(planes - 1 - q, 1 - joined(z) * jnp.abs(side(pz) - side(z)))

            @pl.when(added > 0)
            def _():
                landed(got_x.at[q], x_r.at[q])
                div[q] = got[q] + got_x[q]

            @pl.when(added <= 0)
            def _():
                div[q] = got[q]
        group = pl.ds(y * count_z, count_z)
        pltpu.make_async_copy(div.at[group], div_hbm.at[group], put_sem.at[count_y + i]).start()
        return carry

    lax.fori_loop(0, count_y, collect, 0)

    def finish(k, carry):
        pressure_sends(k, sent)
        forward(k, sent)
        lend(k, sent)
        result_sends(k, sent)
        c = cols(wrap(py + k))
        pltpu.make_async_copy(out.at[:, :, c], out_hbm.at[:, 0, :, c], put_sem.at[k]).wait()
        group = pl.ds(wrap(py - k - 1) * count_z, count_z)
        pltpu.make_async_copy(div.at[group], div_hbm.at[group], put_sem.at[count_y + k]).wait()
        return carry

    edge_sends(sent)
    lax.fori_loop(0, count_y, finish, 0)


def on_device(velocity, fluid, pressure):
    count_y = lax.axis_size("py")
    count_z = lax.axis_size("pz")
    rows, across = fluid.shape[1:]
    planes = pressure.shape[0]
    block = pressure.shape[1:]
    half_rows = (count_z // 2 if count_z % 2 == 0 else 1) * (rows // count_z)
    vm = lambda *shape: pltpu.VMEM(shape, jnp.float32)
    dma = lambda n: pltpu.SemaphoreType.DMA((n,))
    steps = count_y * count_z
    return pl.pallas_call(
        functools.partial(kernel, count_y, count_z),
        out_shape=(
            jax.ShapeDtypeStruct(velocity.shape, jnp.float32),
            jax.ShapeDtypeStruct(pressure.shape, jnp.float32),
        ),
        in_specs=[pl.BlockSpec(memory_space=pl.ANY)] * 3,
        out_specs=(pl.BlockSpec(memory_space=pl.ANY),) * 2,
        scratch_shapes=[
            vm(3, rows, across), vm(rows, across), vm(rows, across), vm(rows, across), vm(rows, across),
            vm(rows, LANES), vm(3, rows, across), vm(rows, across), vm(half_rows, across),
            vm(planes, *block), vm(planes, *block), vm(planes, *block),
            dma(2), dma(2 * count_y),
            dma(steps), dma(steps), dma(steps), dma(steps), dma(count_z), dma(count_z),
            dma(count_y), dma(count_y), dma(count_y), dma(count_y), dma(count_y), dma(count_y),
            dma(steps), dma(planes), dma(steps), dma(planes),
        ],
        compiler_params=pltpu.CompilerParams(
            collective_id=0, has_side_effects=True, vmem_limit_bytes=40 << 20
        ),
        name="project_all",
    )(velocity, fluid, pressure)


def solution(mesh):
    placed = (P(None, ("py", "pz"), None, None), P(("py", "pz"), None, None), P(None, "pz", "py"))
    return jax.shard_map(
        on_device,
        mesh=mesh,
        in_specs=placed,
        out_specs=(P(None, ("py", "pz"), None, None), P(None, "pz", "py")),
        check_vma=False,
    )
```

```python
import functools

import jax
import jax.numpy as jnp
from jax import lax
from jax.experimental import pallas as pl
from jax.experimental.pallas import tpu as pltpu
from jax.sharding import PartitionSpec as P

AHEAD = 2
LANES = 128


def kernel(
    count_y, count_z, v_hbm, f_hbm, p_hbm, out_hbm, div,
    v, f, f_low, main, halo, left, out, part, next_x, got, got_x,
    in_sem, put_sem,
    main_s, main_r, halo_s, halo_r, edge_s, edge_r, f_s, f_r, fwd_s, fwd_r, nx_s, nx_r,
    a_s, a_r, x_s, x_r,
):
    py = lax.axis_index("py")
    pz = lax.axis_index("pz")
    me = py * count_z + pz
    planes = count_y * count_z
    rows, across = f.shape
    width = across // count_y
    part_rows = rows // count_z
    half = count_z // 2 if count_z % 2 == 0 else 1

    def side(z):
        return z // half if isinstance(z, int) else lax.div(z, half)

    def joined(z):
        return min((z + 1) % half, 1) if isinstance(z, int) else jnp.minimum(lax.rem(z + 1, half), 1)

    def cols(c):
        return pl.ds(pl.multiple_of(c * width, width), width)

    def band(g):
        return pl.ds(g * part_rows, part_rows)

    def wrap(c):
        return lax.rem(c + 2 * count_y, count_y)

    def remote(src, dst, send, recv, y, z):
        return pltpu.make_async_remote_copy(
            src_ref=src, dst_ref=dst, send_sem=send, recv_sem=recv,
            device_id=(y, z), device_id_type=pl.DeviceIdType.MESH,
        )

    def begin(src, dst, send, recv, y, z, gate=1, away=False):
        apart = 1 if away else jnp.abs(y * count_z + z - me)

        @pl.when(jnp.minimum(gate, apart) > 0)
        def _():
            remote(src, dst, send, recv, y, z).start()

        if not away:
            @pl.when(gate - jnp.minimum(apart, 1) > 0)
            def _():
                pltpu.make_async_copy(src, dst, recv).start()

    def sent(src, dst, send, recv, y, z, gate=1, away=False):
        apart = 1 if away else jnp.abs(y * count_z + z - me)

        @pl.when(jnp.minimum(gate, apart) > 0)
        def _():
            remote(src, dst, send, recv, y, z).wait_send()

    def landed(dst, recv):
        pltpu.make_async_copy(dst, dst, recv).wait()

    def passed(z, g):
        low, high = (min, max) if isinstance(z, int) and isinstance(g, int) else (jnp.minimum, jnp.maximum)
        apart = low(high(abs(g - z) - 1, 0), 1)
        across_middle = joined(z - 1) * low(abs(side(g) - side(z)), 1)
        return low(high(apart, across_middle), low(z, 1))

    def passed_up(z, g):
        return passed(z + 1, g) if isinstance(z, int) and z < count_z - 1 else (
            0 if isinstance(z, int) else jnp.minimum(passed(z + 1, g), count_z - 1 - z))

    loads = [
        pltpu.make_async_copy(v_hbm.at[:, 0], v, in_sem.at[0]),
        pltpu.make_async_copy(f_hbm.at[0], f, in_sem.at[1]),
    ]
    for load in loads:
        load.start()

    barrier = pltpu.get_barrier_semaphore()

    def greet(i, carry):
        @pl.when(i != me)
        def _():
            pl.semaphore_signal(
                barrier, inc=1, device_id=(lax.div(i, count_z), lax.rem(i, count_z)),
                device_id_type=pl.DeviceIdType.MESH,
            )
        return carry

    lax.fori_loop(0, planes, greet, 0)
    pl.semaphore_wait(barrier, planes - 1)

    mine = pl.ds(pl.multiple_of(pz * part_rows, part_rows), part_rows)
    ahead_y = lax.div(me + 1, count_z)
    ahead_z = lax.rem(me + 1, count_z)

    def pressure_sends(k, do):
        y = wrap(py - k)
        for z in range(count_z):
            target = y * count_z + z
            slot = k * count_z + z
            do(p_hbm.at[target], main.at[mine, cols(py)], main_s.at[slot], main_r.at[k * count_z + pz], y, z)

            do(p_hbm.at[jnp.maximum(target - 1, 0)], halo.at[mine, cols(py)],
               halo_s.at[slot], halo_r.at[k * count_z + pz], y, z, gate=1 - passed(z, pz))
        c = cols(wrap(ahead_y + k))
        do(f_hbm.at[0, :, c], f_low.at[:, c], f_s.at[k], f_r.at[k], ahead_y, ahead_z,
           gate=planes - 1 - me, away=True)

    def edge_sends(do):
        for z in range(count_z):
            y = wrap(py + 1)
            do(p_hbm.at[y * count_z + z, :, width - LANES:], left.at[mine],
               edge_s.at[z], edge_r.at[pz], y, z, away=True)

    def forward(k, do):
        c = cols(wrap(py + k))
        for g in range(count_z):
            slot = k * count_z + g
            do(main.at[band(g), c], halo.at[band(g), c], fwd_s.at[slot], fwd_r.at[slot], py, pz + 1,
               gate=passed_up(pz, g), away=True)

    def lend(k, do):
        c = cols(wrap(py + k))
        for g in range(count_z):
            slot = k * count_z + g
            do(out.at[0, band(g), c], next_x.at[band(g), c], nx_s.at[slot], nx_r.at[slot], py, pz - 1,
               gate=passed(pz, g), away=True)

    def result_sends(k, do):
        y = wrap(py + k)
        for z in range(count_z):
            slot = k * count_z + z
            do(part.at[band(z), cols(y)], got.at[me], a_s.at[slot], a_r.at[me], y, z)
            below = jnp.maximum(me - 1, 0)
            do(out.at[0, band(z), cols(y)], got_x.at[below], x_s.at[slot], x_r.at[below], y, z,
               gate=jnp.minimum(me, 1 - passed(pz, z)))

    edge_sends(begin)
    for k in range(min(AHEAD, count_y)):
        pressure_sends(k, begin)
    for load in loads:
        load.wait()
    for z in range(count_z):
        landed(left.at[band(z)], edge_r.at[z])

    def before(tile, values):
        wide = jnp.concatenate([tile, values], 1)
        return pltpu.roll(wide, 1, 1)[:, LANES:]

    def project(k):
        @pl.when(k + AHEAD < count_y)
        def _():
            pressure_sends(k + AHEAD, begin)

        y = wrap(py + k)
        c = cols(y)
        for z in range(count_z):
            landed(main.at[band(z), c], main_r.at[k * count_z + z])
        forward(k, begin)
        for z in range(count_z):
            @pl.when(passed(pz, z) == 0)
            def _():
                landed(halo.at[band(z), c], halo_r.at[k * count_z + z])

            @pl.when(passed(pz, z) > 0)
            def _():
                landed(halo.at[band(z), c], fwd_r.at[k * count_z + z])

        @pl.when(me > 0)
        def _():
            landed(f_low.at[:, c], f_r.at[k])

        fluid = f[:, c]
        here = main[:, c]
        w_x = 0.5 * (fluid + f_low[:, c])
        along_x = w_x * (v[0, :, c] - (here - halo[:, c]))
        out[0, :, c] = jnp.where(me == 0, jnp.float32(0.0), along_x)
        lend(k, begin)
        z_index = lax.broadcasted_iota(jnp.int32, fluid.shape, 0)
        w_z = 0.5 * (fluid + pltpu.roll(fluid, 1, 0))
        along_z = w_z * (v[1, :, c] - (here - pltpu.roll(here, 1, 0)))
        out[1, :, c] = jnp.where(z_index == 0, jnp.float32(0.0), along_z)
        y_index = lax.broadcasted_iota(jnp.int32, fluid.shape, 1) + y * width
        f_tile = f[:, pl.ds(pl.multiple_of(wrap(y - 1) * width + (width - LANES), LANES), LANES)]
        w_y = 0.5 * (fluid + before(f_tile, fluid))
        along_y = w_y * (v[2, :, c] - (here - before(left[...], here)))
        out[2, :, c] = jnp.where(y_index == 0, jnp.float32(0.0), along_y)
        left[...] = here[:, width - LANES:]
        pltpu.make_async_copy(out.at[:, :, c], out_hbm.at[:, 0, :, c], put_sem.at[k]).start()

    def diverge(k):
        y = wrap(py + k)
        c = cols(y)
        along_z = out[1, :, c]
        along_y = out[2, :, c]
        z_index = lax.broadcasted_iota(jnp.int32, along_z.shape, 0)
        y_index = lax.broadcasted_iota(jnp.int32, along_z.shape, 1) + y * width
        z_next = jnp.where(z_index == rows - 1, jnp.float32(0.0), pltpu.roll(along_z, rows - 1, 0))
        tile = out[2, :, pl.ds(pl.multiple_of(wrap(y + 1) * width, width), LANES)]
        wide = pltpu.roll(jnp.concatenate([along_y, tile], 1), width + LANES - 1, 1)[:, :width]
        y_next = jnp.where(y_index == across - 1, jnp.float32(0.0), wide)
        part[:, c] = (z_next - along_z) + (y_next - along_y) - out[0, :, c]

        for g in range(count_z):
            @pl.when(passed_up(pz, g) > 0)
            def _():
                landed(next_x.at[band(g), c], nx_r.at[k * count_z + g])
                part[band(g), c] = part[band(g), c] + next_x[band(g), c]

        result_sends(k, begin)

    def step(k, carry):
        @pl.when(k < count_y)
        def _():
            project(k)

        @pl.when(k > 0)
        def _():
            diverge(k - 1)
        return carry

    lax.fori_loop(0, count_y + 1, step, 0)

    def collect(i, carry):
        y = wrap(py - i - 1)
        for z in range(count_z):
            q = y * count_z + z
            landed(got.at[q], a_r.at[q])
            added = jnp.minimum(planes - 1 - q, 1 - passed_up(z, pz))

            @pl.when(added > 0)
            def _():
                landed(got_x.at[q], x_r.at[q])
                div[q] = got[q] + got_x[q]

            @pl.when(added <= 0)
            def _():
                div[q] = got[q]
        return carry

    lax.fori_loop(0, count_y, collect, 0)

    def finish(k, carry):
        pressure_sends(k, sent)
        forward(k, sent)
        lend(k, sent)
        result_sends(k, sent)
        c = cols(wrap(py + k))
        pltpu.make_async_copy(out.at[:, :, c], out_hbm.at[:, 0, :, c], put_sem.at[k]).wait()
        return carry

    edge_sends(sent)
    lax.fori_loop(0, count_y, finish, 0)


def on_device(velocity, fluid, pressure):
    count_y = lax.axis_size("py")
    count_z = lax.axis_size("pz")
    rows, across = fluid.shape[1:]
    planes = pressure.shape[0]
    block = pressure.shape[1:]
    vm = lambda *shape: pltpu.VMEM(shape, jnp.float32)
    dma = lambda n: pltpu.SemaphoreType.DMA((n,))
    steps = count_y * count_z
    return pl.pallas_call(
        functools.partial(kernel, count_y, count_z),
        out_shape=(
            jax.ShapeDtypeStruct(velocity.shape, jnp.float32),
            jax.ShapeDtypeStruct(pressure.shape, jnp.float32),
        ),
        in_specs=[pl.BlockSpec(memory_space=pltpu.MemorySpace.HBM)] * 3,
        out_specs=(pl.BlockSpec(memory_space=pl.ANY), pl.BlockSpec(memory_space=pltpu.VMEM)),
        scratch_shapes=[
            vm(3, rows, across), vm(rows, across), vm(rows, across), vm(rows, across), vm(rows, across),
            vm(rows, LANES), vm(3, rows, across), vm(rows, across), vm(rows, across),
            vm(planes, *block), vm(planes, *block), dma(2), dma(count_y),
            dma(steps), dma(steps), dma(steps), dma(steps), dma(count_z), dma(count_z),
            dma(count_y), dma(count_y), dma(steps), dma(steps), dma(steps), dma(steps),
            dma(steps), dma(planes), dma(steps), dma(planes),
        ],
        compiler_params=pltpu.CompilerParams(
            collective_id=0, has_side_effects=True, vmem_limit_bytes=52 << 20
        ),
        name="project_all",
    )(velocity, fluid, pressure)


def solution(mesh):
    placed = (P(None, ("py", "pz"), None, None), P(("py", "pz"), None, None), P(None, "pz", "py"))
    return jax.shard_map(
        on_device,
        mesh=mesh,
        in_specs=placed,
        out_specs=(P(None, ("py", "pz"), None, None), P(None, "pz", "py")),
        check_vma=False,
    )
```

```python
import functools

import jax
import jax.numpy as jnp
from jax import lax
from jax.experimental import pallas as pl
from jax.experimental.pallas import tpu as pltpu
from jax.sharding import PartitionSpec as P

AHEAD = 2
LANES = 128


def kernel(
    count_y, count_z, v_hbm, f_hbm, p_hbm, out_ref, div,
    v, f, f_low, main, halo, left, part, next_x, got, got_x,
    in_sem,
    main_s, main_r, halo_s, halo_r, edge_s, edge_r, f_s, f_r, fwd_s, fwd_r, nx_s, nx_r,
    a_s, a_r, x_s, x_r,
):
    out = out_ref.at[:, 0]
    py = lax.axis_index("py")
    pz = lax.axis_index("pz")
    me = py * count_z + pz
    planes = count_y * count_z
    rows, across = f.shape
    width = across // count_y
    part_rows = rows // count_z
    half = count_z // 2 if count_z % 2 == 0 else 1

    def side(z):
        return z // half if isinstance(z, int) else lax.div(z, half)

    def joined(z):
        return min((z + 1) % half, 1) if isinstance(z, int) else jnp.minimum(lax.rem(z + 1, half), 1)

    def cols(c):
        return pl.ds(pl.multiple_of(c * width, width), width)

    def band(g):
        return pl.ds(g * part_rows, part_rows)

    def wrap(c):
        return lax.rem(c + 2 * count_y, count_y)

    def remote(src, dst, send, recv, y, z):
        return pltpu.make_async_remote_copy(
            src_ref=src, dst_ref=dst, send_sem=send, recv_sem=recv,
            device_id=(y, z), device_id_type=pl.DeviceIdType.MESH,
        )

    def begin(src, dst, send, recv, y, z, gate=1, away=False):
        apart = 1 if away else jnp.abs(y * count_z + z - me)

        @pl.when(jnp.minimum(gate, apart) > 0)
        def _():
            remote(src, dst, send, recv, y, z).start()

        if not away:
            @pl.when(gate - jnp.minimum(apart, 1) > 0)
            def _():
                pltpu.make_async_copy(src, dst, recv).start()

    def sent(src, dst, send, recv, y, z, gate=1, away=False):
        apart = 1 if away else jnp.abs(y * count_z + z - me)

        @pl.when(jnp.minimum(gate, apart) > 0)
        def _():
            remote(src, dst, send, recv, y, z).wait_send()

    def landed(dst, recv):
        pltpu.make_async_copy(dst, dst, recv).wait()

    def passed(z, g):
        low, high = (min, max) if isinstance(z, int) and isinstance(g, int) else (jnp.minimum, jnp.maximum)
        apart = low(high(abs(g - z) - 1, 0), 1)
        across_middle = joined(z - 1) * low(abs(side(g) - side(z)), 1)
        return low(high(apart, across_middle), low(z, 1))

    def passed_up(z, g):
        return passed(z + 1, g) if isinstance(z, int) and z < count_z - 1 else (
            0 if isinstance(z, int) else jnp.minimum(passed(z + 1, g), count_z - 1 - z))

    loads = [
        pltpu.make_async_copy(v_hbm.at[:, 0], v, in_sem.at[0]),
        pltpu.make_async_copy(f_hbm.at[0], f, in_sem.at[1]),
    ]
    for load in loads:
        load.start()

    barrier = pltpu.get_barrier_semaphore()

    def greet(i, carry):
        @pl.when(i != me)
        def _():
            pl.semaphore_signal(
                barrier, inc=1, device_id=(lax.div(i, count_z), lax.rem(i, count_z)),
                device_id_type=pl.DeviceIdType.MESH,
            )
        return carry

    lax.fori_loop(0, planes, greet, 0)
    pl.semaphore_wait(barrier, planes - 1)

    mine = pl.ds(pl.multiple_of(pz * part_rows, part_rows), part_rows)
    ahead_y = lax.div(me + 1, count_z)
    ahead_z = lax.rem(me + 1, count_z)

    def pressure_sends(k, do):
        y = wrap(py - k)
        for z in range(count_z):
            target = y * count_z + z
            slot = k * count_z + z
            do(p_hbm.at[target], main.at[mine, cols(py)], main_s.at[slot], main_r.at[k * count_z + pz], y, z)

            do(p_hbm.at[jnp.maximum(target - 1, 0)], halo.at[mine, cols(py)],
               halo_s.at[slot], halo_r.at[k * count_z + pz], y, z, gate=1 - passed(z, pz))
        c = cols(wrap(ahead_y + k))
        do(f_hbm.at[0, :, c], f_low.at[:, c], f_s.at[k], f_r.at[k], ahead_y, ahead_z,
           gate=planes - 1 - me, away=True)

    def edge_sends(do):
        for z in range(count_z):
            y = wrap(py + 1)
            do(p_hbm.at[y * count_z + z, :, width - LANES:], left.at[mine],
               edge_s.at[z], edge_r.at[pz], y, z, away=True)

    def forward(k, do):
        c = cols(wrap(py + k))
        for g in range(count_z):
            slot = k * count_z + g
            do(main.at[band(g), c], halo.at[band(g), c], fwd_s.at[slot], fwd_r.at[slot], py, pz + 1,
               gate=passed_up(pz, g), away=True)

    def lend(k, do):
        c = cols(wrap(py + k))
        for g in range(count_z):
            slot = k * count_z + g
            do(out.at[0, band(g), c], next_x.at[band(g), c], nx_s.at[slot], nx_r.at[slot], py, pz - 1,
               gate=passed(pz, g), away=True)

    def result_sends(k, do):
        y = wrap(py + k)
        for z in range(count_z):
            slot = k * count_z + z
            do(part.at[band(z), cols(y)], got.at[me], a_s.at[slot], a_r.at[me], y, z)
            below = jnp.maximum(me - 1, 0)
            do(out.at[0, band(z), cols(y)], got_x.at[below], x_s.at[slot], x_r.at[below], y, z,
               gate=jnp.minimum(me, 1 - passed(pz, z)))

    edge_sends(begin)
    for k in range(min(AHEAD, count_y)):
        pressure_sends(k, begin)
    for load in loads:
        load.wait()
    for z in range(count_z):
        landed(left.at[band(z)], edge_r.at[z])

    def before(tile, values):
        wide = jnp.concatenate([tile, values], 1)
        return pltpu.roll(wide, 1, 1)[:, LANES:]

    def project(k):
        @pl.when(k + AHEAD < count_y)
        def _():
            pressure_sends(k + AHEAD, begin)

        y = wrap(py + k)
        c = cols(y)
        for z in range(count_z):
            landed(main.at[band(z), c], main_r.at[k * count_z + z])
        forward(k, begin)
        for z in range(count_z):
            @pl.when(passed(pz, z) == 0)
            def _():
                landed(halo.at[band(z), c], halo_r.at[k * count_z + z])

            @pl.when(passed(pz, z) > 0)
            def _():
                landed(halo.at[band(z), c], fwd_r.at[k * count_z + z])

        @pl.when(me > 0)
        def _():
            landed(f_low.at[:, c], f_r.at[k])

        fluid = f[:, c]
        here = main[:, c]
        w_x = 0.5 * (fluid + f_low[:, c])
        along_x = w_x * (v[0, :, c] - (here - halo[:, c]))
        out[0, :, c] = jnp.where(me == 0, jnp.float32(0.0), along_x)
        lend(k, begin)
        z_index = lax.broadcasted_iota(jnp.int32, fluid.shape, 0)
        w_z = 0.5 * (fluid + pltpu.roll(fluid, 1, 0))
        along_z = w_z * (v[1, :, c] - (here - pltpu.roll(here, 1, 0)))
        out[1, :, c] = jnp.where(z_index == 0, jnp.float32(0.0), along_z)
        y_index = lax.broadcasted_iota(jnp.int32, fluid.shape, 1) + y * width
        f_tile = f[:, pl.ds(pl.multiple_of(wrap(y - 1) * width + (width - LANES), LANES), LANES)]
        w_y = 0.5 * (fluid + before(f_tile, fluid))
        along_y = w_y * (v[2, :, c] - (here - before(left[...], here)))
        out[2, :, c] = jnp.where(y_index == 0, jnp.float32(0.0), along_y)
        left[...] = here[:, width - LANES:]

    def diverge(k):
        y = wrap(py + k)
        c = cols(y)
        along_z = out[1, :, c]
        along_y = out[2, :, c]
        z_index = lax.broadcasted_iota(jnp.int32, along_z.shape, 0)
        y_index = lax.broadcasted_iota(jnp.int32, along_z.shape, 1) + y * width
        z_next = jnp.where(z_index == rows - 1, jnp.float32(0.0), pltpu.roll(along_z, rows - 1, 0))
        tile = out[2, :, pl.ds(pl.multiple_of(wrap(y + 1) * width, width), LANES)]
        wide = pltpu.roll(jnp.concatenate([along_y, tile], 1), width + LANES - 1, 1)[:, :width]
        y_next = jnp.where(y_index == across - 1, jnp.float32(0.0), wide)
        part[:, c] = (z_next - along_z) + (y_next - along_y) - out[0, :, c]

        for g in range(count_z):
            @pl.when(passed_up(pz, g) > 0)
            def _():
                landed(next_x.at[band(g), c], nx_r.at[k * count_z + g])
                part[band(g), c] = part[band(g), c] + next_x[band(g), c]

        result_sends(k, begin)

    def step(k, carry):
        @pl.when(k < count_y)
        def _():
            project(k)

        @pl.when(k > 0)
        def _():
            diverge(k - 1)
        return carry

    lax.fori_loop(0, count_y + 1, step, 0)

    def collect(i, carry):
        y = wrap(py - i - 1)
        for z in range(count_z):
            q = y * count_z + z
            landed(got.at[q], a_r.at[q])
            added = jnp.minimum(planes - 1 - q, 1 - passed_up(z, pz))

            @pl.when(added > 0)
            def _():
                landed(got_x.at[q], x_r.at[q])
                div[q] = got[q] + got_x[q]

            @pl.when(added <= 0)
            def _():
                div[q] = got[q]
        return carry

    lax.fori_loop(0, count_y, collect, 0)

    def finish(k, carry):
        pressure_sends(k, sent)
        forward(k, sent)
        lend(k, sent)
        result_sends(k, sent)
        return carry

    edge_sends(sent)
    lax.fori_loop(0, count_y, finish, 0)


def on_device(velocity, fluid, pressure):
    count_y = lax.axis_size("py")
    count_z = lax.axis_size("pz")
    rows, across = fluid.shape[1:]
    planes = pressure.shape[0]
    block = pressure.shape[1:]
    vm = lambda *shape: pltpu.VMEM(shape, jnp.float32)
    dma = lambda n: pltpu.SemaphoreType.DMA((n,))
    steps = count_y * count_z
    return pl.pallas_call(
        functools.partial(kernel, count_y, count_z),
        out_shape=(
            jax.ShapeDtypeStruct(velocity.shape, jnp.float32),
            jax.ShapeDtypeStruct(pressure.shape, jnp.float32),
        ),
        in_specs=[pl.BlockSpec(memory_space=pltpu.MemorySpace.HBM)] * 3,
        out_specs=(pl.BlockSpec(memory_space=pltpu.VMEM),) * 2,
        scratch_shapes=[
            vm(3, rows, across), vm(rows, across), vm(rows, across), vm(rows, across), vm(rows, across),
            vm(rows, LANES), vm(rows, across), vm(rows, across),
            vm(planes, *block), vm(planes, *block), dma(2),
            dma(steps), dma(steps), dma(steps), dma(steps), dma(count_z), dma(count_z),
            dma(count_y), dma(count_y), dma(steps), dma(steps), dma(steps), dma(steps),
            dma(steps), dma(planes), dma(steps), dma(planes),
        ],
        compiler_params=pltpu.CompilerParams(
            collective_id=0, has_side_effects=True, vmem_limit_bytes=40 << 20
        ),
        name="project_all",
    )(*(pltpu.with_memory_space_constraint(x, pltpu.MemorySpace.HBM) for x in (velocity, fluid, pressure)))


def solution(mesh):
    placed = (P(None, ("py", "pz"), None, None), P(("py", "pz"), None, None), P(None, "pz", "py"))
    return jax.shard_map(
        on_device,
        mesh=mesh,
        in_specs=placed,
        out_specs=(P(None, ("py", "pz"), None, None), P(None, "pz", "py")),
        check_vma=False,
    )
```

```python
import functools

import jax
import jax.numpy as jnp
from jax import lax
from jax.experimental import pallas as pl
from jax.experimental.pallas import tpu as pltpu
from jax.sharding import PartitionSpec as P

AHEAD = 2
LANES = 128


def kernel(
    count_y, count_z, v_hbm, f_hbm, p_hbm, out_ref, div,
    v, f, f_low, main, halo, left, tail, packed, edge, part, next_x, got, got_x,
    in_sem,
    main_s, main_r, halo_s, halo_r, edge_s, edge_r, f_s, f_r, fwd_s, fwd_r, nx_s, nx_r,
    a_s, a_r, x_s, x_r,
):
    out = out_ref.at[:, 0]
    py = lax.axis_index("py")
    pz = lax.axis_index("pz")
    me = py * count_z + pz
    planes = count_y * count_z
    rows, across = f.shape
    width = across // count_y
    part_rows = rows // count_z
    half = count_z // 2 if count_z % 2 == 0 else 1

    def side(z):
        return z // half if isinstance(z, int) else lax.div(z, half)

    def joined(z):
        return min((z + 1) % half, 1) if isinstance(z, int) else jnp.minimum(lax.rem(z + 1, half), 1)

    def cols(c):
        return pl.ds(pl.multiple_of(c * width, width), width)

    def band(g):
        return pl.ds(g * part_rows, part_rows)

    def wrap(c):
        return lax.rem(c + 2 * count_y, count_y)

    def remote(src, dst, send, recv, y, z):
        return pltpu.make_async_remote_copy(
            src_ref=src, dst_ref=dst, send_sem=send, recv_sem=recv,
            device_id=(y, z), device_id_type=pl.DeviceIdType.MESH,
        )

    def begin(src, dst, send, recv, y, z, gate=1, away=False):
        apart = 1 if away else jnp.abs(y * count_z + z - me)

        @pl.when(jnp.minimum(gate, apart) > 0)
        def _():
            remote(src, dst, send, recv, y, z).start()

        if not away:
            @pl.when(gate - jnp.minimum(apart, 1) > 0)
            def _():
                pltpu.make_async_copy(src, dst, recv).start()

    def sent(src, dst, send, recv, y, z, gate=1, away=False):
        apart = 1 if away else jnp.abs(y * count_z + z - me)

        @pl.when(jnp.minimum(gate, apart) > 0)
        def _():
            remote(src, dst, send, recv, y, z).wait_send()

    def landed(dst, recv):
        pltpu.make_async_copy(dst, dst, recv).wait()

    def passed(z, g):
        low, high = (min, max) if isinstance(z, int) and isinstance(g, int) else (jnp.minimum, jnp.maximum)
        apart = low(high(abs(g - z) - 1, 0), 1)
        across_middle = joined(z - 1) * low(abs(side(g) - side(z)), 1)
        return low(high(apart, across_middle), low(z, 1))

    def passed_up(z, g):
        return passed(z + 1, g) if isinstance(z, int) and z < count_z - 1 else (
            0 if isinstance(z, int) else jnp.minimum(passed(z + 1, g), count_z - 1 - z))

    loads = [
        pltpu.make_async_copy(v_hbm.at[:, 0], v, in_sem.at[0]),
        pltpu.make_async_copy(f_hbm.at[0], f, in_sem.at[1]),
    ]
    next_line = pl.ds(wrap(py + 1) * count_z, count_z)
    loads.append(pltpu.make_async_copy(p_hbm.at[next_line, :, width - LANES:], tail, in_sem.at[2]))
    for load in loads:
        load.start()
    loads[2].wait()
    lane = lax.broadcasted_iota(jnp.int32, (8, LANES), 1)
    for z in range(count_z):
        tile = jnp.zeros((8, LANES), jnp.float32)
        for i in range(part_rows // 8):
            column = jnp.broadcast_to(tail[z, 8 * i:8 * i + 8, LANES - 1:], (8, LANES))
            tile = jnp.where(lane == i, column, tile)
        packed[z] = tile

    barrier = pltpu.get_barrier_semaphore()

    def greet(i, carry):
        @pl.when(i != me)
        def _():
            pl.semaphore_signal(
                barrier, inc=1, device_id=(lax.div(i, count_z), lax.rem(i, count_z)),
                device_id_type=pl.DeviceIdType.MESH,
            )
        return carry

    lax.fori_loop(0, planes, greet, 0)
    pl.semaphore_wait(barrier, planes - 1)

    mine = pl.ds(pl.multiple_of(pz * part_rows, part_rows), part_rows)
    ahead_y = lax.div(me + 1, count_z)
    ahead_z = lax.rem(me + 1, count_z)

    def pressure_sends(k, do):
        y = wrap(py - k)
        for z in range(count_z):
            target = y * count_z + z
            slot = k * count_z + z
            do(p_hbm.at[target], main.at[mine, cols(py)], main_s.at[slot], main_r.at[k * count_z + pz], y, z)

            do(p_hbm.at[jnp.maximum(target - 1, 0)], halo.at[mine, cols(py)],
               halo_s.at[slot], halo_r.at[k * count_z + pz], y, z, gate=1 - passed(z, pz))
        c = cols(wrap(ahead_y + k))
        do(f_hbm.at[0, :, c], f_low.at[:, c], f_s.at[k], f_r.at[k], ahead_y, ahead_z,
           gate=planes - 1 - me, away=True)

    def edge_sends(do):
        for z in range(count_z):
            y = wrap(py + 1)
            do(packed.at[z], edge.at[pz], edge_s.at[z], edge_r.at[pz], y, z, away=True)

    def forward(k, do):
        c = cols(wrap(py + k))
        for g in range(count_z):
            slot = k * count_z + g
            do(main.at[band(g), c], halo.at[band(g), c], fwd_s.at[slot], fwd_r.at[slot], py, pz + 1,
               gate=passed_up(pz, g), away=True)

    def lend(k, do):
        c = cols(wrap(py + k))
        for g in range(count_z):
            slot = k * count_z + g
            do(out.at[0, band(g), c], next_x.at[band(g), c], nx_s.at[slot], nx_r.at[slot], py, pz - 1,
               gate=passed(pz, g), away=True)

    def result_sends(k, do):
        y = wrap(py + k)
        for z in range(count_z):
            slot = k * count_z + z
            do(part.at[band(z), cols(y)], got.at[me], a_s.at[slot], a_r.at[me], y, z)
            below = jnp.maximum(me - 1, 0)
            do(out.at[0, band(z), cols(y)], got_x.at[below], x_s.at[slot], x_r.at[below], y, z,
               gate=jnp.minimum(me, 1 - passed(pz, z)))

    for k in range(min(AHEAD, count_y)):
        pressure_sends(k, begin)
        if k == 0:
            edge_sends(begin)
    for z in range(count_z):
        landed(edge.at[z], edge_r.at[z])
        for i in range(part_rows // 8):
            rows_at = z * part_rows + 8 * i
            left[rows_at:rows_at + 8] = jnp.broadcast_to(edge[z, :, i:i + 1], (8, LANES))
    for load in loads[:2]:
        load.wait()

    def before(tile, values):
        wide = jnp.concatenate([tile, values], 1)
        return pltpu.roll(wide, 1, 1)[:, LANES:]

    def project(k):
        @pl.when(k + AHEAD < count_y)
        def _():
            pressure_sends(k + AHEAD, begin)

        y = wrap(py + k)
        c = cols(y)
        for z in range(count_z):
            landed(main.at[band(z), c], main_r.at[k * count_z + z])
        forward(k, begin)
        for z in range(count_z):
            @pl.when(passed(pz, z) == 0)
            def _():
                landed(halo.at[band(z), c], halo_r.at[k * count_z + z])

            @pl.when(passed(pz, z) > 0)
            def _():
                landed(halo.at[band(z), c], fwd_r.at[k * count_z + z])

        @pl.when(me > 0)
        def _():
            landed(f_low.at[:, c], f_r.at[k])

        fluid = f[:, c]
        here = main[:, c]
        w_x = 0.5 * (fluid + f_low[:, c])
        along_x = w_x * (v[0, :, c] - (here - halo[:, c]))
        out[0, :, c] = jnp.where(me == 0, jnp.float32(0.0), along_x)
        lend(k, begin)
        z_index = lax.broadcasted_iota(jnp.int32, fluid.shape, 0)
        w_z = 0.5 * (fluid + pltpu.roll(fluid, 1, 0))
        along_z = w_z * (v[1, :, c] - (here - pltpu.roll(here, 1, 0)))
        out[1, :, c] = jnp.where(z_index == 0, jnp.float32(0.0), along_z)
        y_index = lax.broadcasted_iota(jnp.int32, fluid.shape, 1) + y * width
        f_tile = f[:, pl.ds(pl.multiple_of(wrap(y - 1) * width + (width - LANES), LANES), LANES)]
        w_y = 0.5 * (fluid + before(f_tile, fluid))
        along_y = w_y * (v[2, :, c] - (here - before(left[...], here)))
        out[2, :, c] = jnp.where(y_index == 0, jnp.float32(0.0), along_y)
        left[...] = here[:, width - LANES:]

    def diverge(k):
        y = wrap(py + k)
        c = cols(y)
        along_z = out[1, :, c]
        along_y = out[2, :, c]
        z_index = lax.broadcasted_iota(jnp.int32, along_z.shape, 0)
        y_index = lax.broadcasted_iota(jnp.int32, along_z.shape, 1) + y * width
        z_next = jnp.where(z_index == rows - 1, jnp.float32(0.0), pltpu.roll(along_z, rows - 1, 0))
        tile = out[2, :, pl.ds(pl.multiple_of(wrap(y + 1) * width, width), LANES)]
        wide = pltpu.roll(jnp.concatenate([along_y, tile], 1), width + LANES - 1, 1)[:, :width]
        y_next = jnp.where(y_index == across - 1, jnp.float32(0.0), wide)
        part[:, c] = (z_next - along_z) + (y_next - along_y) - out[0, :, c]

        for g in range(count_z):
            @pl.when(passed_up(pz, g) > 0)
            def _():
                landed(next_x.at[band(g), c], nx_r.at[k * count_z + g])
                part[band(g), c] = part[band(g), c] + next_x[band(g), c]

        result_sends(k, begin)

    def step(k, carry):
        @pl.when(k < count_y)
        def _():
            project(k)

        @pl.when(k > 0)
        def _():
            diverge(k - 1)
        return carry

    lax.fori_loop(0, count_y + 1, step, 0)

    def collect(i, carry):
        y = wrap(py - i - 1)
        for z in range(count_z):
            q = y * count_z + z
            landed(got.at[q], a_r.at[q])
            added = jnp.minimum(planes - 1 - q, 1 - passed_up(z, pz))

            @pl.when(added > 0)
            def _():
                landed(got_x.at[q], x_r.at[q])
                div[q] = got[q] + got_x[q]

            @pl.when(added <= 0)
            def _():
                div[q] = got[q]
        return carry

    lax.fori_loop(0, count_y, collect, 0)

    def finish(k, carry):
        pressure_sends(k, sent)
        forward(k, sent)
        lend(k, sent)
        result_sends(k, sent)
        return carry

    edge_sends(sent)
    lax.fori_loop(0, count_y, finish, 0)


def on_device(velocity, fluid, pressure):
    count_y = lax.axis_size("py")
    count_z = lax.axis_size("pz")
    rows, across = fluid.shape[1:]
    planes = pressure.shape[0]
    block = pressure.shape[1:]
    vm = lambda *shape: pltpu.VMEM(shape, jnp.float32)
    dma = lambda n: pltpu.SemaphoreType.DMA((n,))
    steps = count_y * count_z
    return pl.pallas_call(
        functools.partial(kernel, count_y, count_z),
        out_shape=(
            jax.ShapeDtypeStruct(velocity.shape, jnp.float32),
            jax.ShapeDtypeStruct(pressure.shape, jnp.float32),
        ),
        in_specs=[pl.BlockSpec(memory_space=pltpu.MemorySpace.HBM)] * 3,
        out_specs=(pl.BlockSpec(memory_space=pltpu.VMEM),) * 2,
        scratch_shapes=[
            vm(3, rows, across), vm(rows, across), vm(rows, across), vm(rows, across), vm(rows, across),
            vm(rows, LANES), vm(count_z, block[0], LANES), vm(count_z, 8, LANES), vm(count_z, 8, LANES),
            vm(rows, across), vm(rows, across),
            vm(planes, *block), vm(planes, *block), dma(3),
            dma(steps), dma(steps), dma(steps), dma(steps), dma(count_z), dma(count_z),
            dma(count_y), dma(count_y), dma(steps), dma(steps), dma(steps), dma(steps),
            dma(steps), dma(planes), dma(steps), dma(planes),
        ],
        compiler_params=pltpu.CompilerParams(
            collective_id=0, has_side_effects=True, vmem_limit_bytes=40 << 20
        ),
        name="project_all",
    )(*(pltpu.with_memory_space_constraint(x, pltpu.MemorySpace.HBM) for x in (velocity, fluid, pressure)))


def solution(mesh):
    placed = (P(None, ("py", "pz"), None, None), P(("py", "pz"), None, None), P(None, "pz", "py"))
    return jax.shard_map(
        on_device,
        mesh=mesh,
        in_specs=placed,
        out_specs=(P(None, ("py", "pz"), None, None), P(None, "pz", "py")),
        check_vma=False,
    )
```

```python
import functools

import jax
import jax.numpy as jnp
from jax import lax
from jax.experimental import pallas as pl
from jax.experimental.pallas import tpu as pltpu
from jax.sharding import PartitionSpec as P

AHEAD = 2
AHEAD_F = 1
LANES = 128


def kernel(
    count_y, count_z, v_hbm, f_hbm, p_hbm, out_ref, div,
    v, f, f_low, main, halo, left, part, next_x, got, got_x,
    in_sem,
    main_s, main_r, halo_s, halo_r, edge_s, edge_r, f_s, f_r, fwd_s, fwd_r, nx_s, nx_r,
    a_s, a_r, x_s, x_r,
):
    out = out_ref.at[:, 0]
    py = lax.axis_index("py")
    pz = lax.axis_index("pz")
    me = py * count_z + pz
    planes = count_y * count_z
    rows, across = f.shape
    width = across // count_y
    part_rows = rows // count_z
    half = count_z // 2 if count_z % 2 == 0 else 1

    def side(z):
        return z // half if isinstance(z, int) else lax.div(z, half)

    def joined(z):
        return min((z + 1) % half, 1) if isinstance(z, int) else jnp.minimum(lax.rem(z + 1, half), 1)

    def cols(c):
        return pl.ds(pl.multiple_of(c * width, width), width)

    def band(g):
        return pl.ds(g * part_rows, part_rows)

    def wrap(c):
        return lax.rem(c + 2 * count_y, count_y)

    def remote(src, dst, send, recv, y, z):
        return pltpu.make_async_remote_copy(
            src_ref=src, dst_ref=dst, send_sem=send, recv_sem=recv,
            device_id=(y, z), device_id_type=pl.DeviceIdType.MESH,
        )

    def begin(src, dst, send, recv, y, z, gate=1, away=False):
        apart = 1 if away else jnp.abs(y * count_z + z - me)

        @pl.when(jnp.minimum(gate, apart) > 0)
        def _():
            remote(src, dst, send, recv, y, z).start()

        if not away:
            @pl.when(gate - jnp.minimum(apart, 1) > 0)
            def _():
                pltpu.make_async_copy(src, dst, recv).start()

    def sent(src, dst, send, recv, y, z, gate=1, away=False):
        apart = 1 if away else jnp.abs(y * count_z + z - me)

        @pl.when(jnp.minimum(gate, apart) > 0)
        def _():
            remote(src, dst, send, recv, y, z).wait_send()

    def landed(dst, recv):
        pltpu.make_async_copy(dst, dst, recv).wait()

    def passed(z, g):
        low, high = (min, max) if isinstance(z, int) and isinstance(g, int) else (jnp.minimum, jnp.maximum)
        apart = low(high(abs(g - z) - 1, 0), 1)
        across_middle = joined(z - 1) * low(abs(side(g) - side(z)), 1)
        return low(high(apart, across_middle), low(z, 1))

    def passed_up(z, g):
        return passed(z + 1, g) if isinstance(z, int) and z < count_z - 1 else (
            0 if isinstance(z, int) else jnp.minimum(passed(z + 1, g), count_z - 1 - z))

    loads = [
        pltpu.make_async_copy(v_hbm.at[:, 0], v, in_sem.at[0]),
        pltpu.make_async_copy(f_hbm.at[0], f, in_sem.at[1]),
    ]
    for load in loads:
        load.start()

    barrier = pltpu.get_barrier_semaphore()

    def greet(i, carry):
        @pl.when(i != me)
        def _():
            pl.semaphore_signal(
                barrier, inc=1, device_id=(lax.div(i, count_z), lax.rem(i, count_z)),
                device_id_type=pl.DeviceIdType.MESH,
            )
        return carry

    lax.fori_loop(0, planes, greet, 0)
    pl.semaphore_wait(barrier, planes - 1)

    mine = pl.ds(pl.multiple_of(pz * part_rows, part_rows), part_rows)
    ahead_y = lax.div(me + 1, count_z)
    ahead_z = lax.rem(me + 1, count_z)

    def pressure_sends(k, do):
        y = wrap(py - k)
        for z in range(count_z):
            target = y * count_z + z
            slot = k * count_z + z
            do(p_hbm.at[target], main.at[mine, cols(py)], main_s.at[slot], main_r.at[k * count_z + pz], y, z)

            do(p_hbm.at[jnp.maximum(target - 1, 0)], halo.at[mine, cols(py)],
               halo_s.at[slot], halo_r.at[k * count_z + pz], y, z, gate=1 - passed(z, pz))

    def fluid_sends(k, do):
        c = cols(wrap(ahead_y + k))
        do(f_hbm.at[0, :, c], f_low.at[:, c], f_s.at[k], f_r.at[k], ahead_y, ahead_z,
           gate=planes - 1 - me, away=True)

    def edge_sends(do):
        for z in range(count_z):
            y = wrap(py + 1)
            do(p_hbm.at[y * count_z + z, :, width - LANES:], left.at[mine],
               edge_s.at[z], edge_r.at[pz], y, z, away=True)

    def forward(k, do):
        c = cols(wrap(py + k))
        for g in range(count_z):
            slot = k * count_z + g
            do(main.at[band(g), c], halo.at[band(g), c], fwd_s.at[slot], fwd_r.at[slot], py, pz + 1,
               gate=passed_up(pz, g), away=True)

    def lend(k, do):
        c = cols(wrap(py + k))
        for g in range(count_z):
            slot = k * count_z + g
            do(out.at[0, band(g), c], next_x.at[band(g), c], nx_s.at[slot], nx_r.at[slot], py, pz - 1,
               gate=passed(pz, g), away=True)

    def result_sends(k, do):
        y = wrap(py + k)
        for z in range(count_z):
            slot = k * count_z + z
            do(part.at[band(z), cols(y)], got.at[me], a_s.at[slot], a_r.at[me], y, z)
            below = jnp.maximum(me - 1, 0)
            do(out.at[0, band(z), cols(y)], got_x.at[below], x_s.at[slot], x_r.at[below], y, z,
               gate=jnp.minimum(me, 1 - passed(pz, z)))

    edge_sends(begin)
    for k in range(min(AHEAD, count_y)):
        pressure_sends(k, begin)
    for k in range(min(AHEAD_F, count_y)):
        fluid_sends(k, begin)
    for load in loads:
        load.wait()
    for z in range(count_z):
        landed(left.at[band(z)], edge_r.at[z])

    def before(tile, values):
        wide = jnp.concatenate([tile, values], 1)
        return pltpu.roll(wide, 1, 1)[:, LANES:]

    def project(k):
        @pl.when(k + AHEAD < count_y)
        def _():
            pressure_sends(k + AHEAD, begin)

        @pl.when(k + AHEAD_F < count_y)
        def _():
            fluid_sends(k + AHEAD_F, begin)

        y = wrap(py + k)
        c = cols(y)
        for z in range(count_z):
            landed(main.at[band(z), c], main_r.at[k * count_z + z])
        forward(k, begin)
        for z in range(count_z):
            @pl.when(passed(pz, z) == 0)
            def _():
                landed(halo.at[band(z), c], halo_r.at[k * count_z + z])

            @pl.when(passed(pz, z) > 0)
            def _():
                landed(halo.at[band(z), c], fwd_r.at[k * count_z + z])

        @pl.when(me > 0)
        def _():
            landed(f_low.at[:, c], f_r.at[k])

        fluid = f[:, c]
        here = main[:, c]
        w_x = 0.5 * (fluid + f_low[:, c])
        along_x = w_x * (v[0, :, c] - (here - halo[:, c]))
        out[0, :, c] = jnp.where(me == 0, jnp.float32(0.0), along_x)
        lend(k, begin)
        z_index = lax.broadcasted_iota(jnp.int32, fluid.shape, 0)
        w_z = 0.5 * (fluid + pltpu.roll(fluid, 1, 0))
        along_z = w_z * (v[1, :, c] - (here - pltpu.roll(here, 1, 0)))
        out[1, :, c] = jnp.where(z_index == 0, jnp.float32(0.0), along_z)
        y_index = lax.broadcasted_iota(jnp.int32, fluid.shape, 1) + y * width
        f_tile = f[:, pl.ds(pl.multiple_of(wrap(y - 1) * width + (width - LANES), LANES), LANES)]
        w_y = 0.5 * (fluid + before(f_tile, fluid))
        along_y = w_y * (v[2, :, c] - (here - before(left[...], here)))
        out[2, :, c] = jnp.where(y_index == 0, jnp.float32(0.0), along_y)
        left[...] = here[:, width - LANES:]

    def diverge(k):
        y = wrap(py + k)
        c = cols(y)
        along_z = out[1, :, c]
        along_y = out[2, :, c]
        z_index = lax.broadcasted_iota(jnp.int32, along_z.shape, 0)
        y_index = lax.broadcasted_iota(jnp.int32, along_z.shape, 1) + y * width
        z_next = jnp.where(z_index == rows - 1, jnp.float32(0.0), pltpu.roll(along_z, rows - 1, 0))
        tile = out[2, :, pl.ds(pl.multiple_of(wrap(y + 1) * width, width), LANES)]
        wide = pltpu.roll(jnp.concatenate([along_y, tile], 1), width + LANES - 1, 1)[:, :width]
        y_next = jnp.where(y_index == across - 1, jnp.float32(0.0), wide)
        part[:, c] = (z_next - along_z) + (y_next - along_y) - out[0, :, c]

        for g in range(count_z):
            @pl.when(passed_up(pz, g) > 0)
            def _():
                landed(next_x.at[band(g), c], nx_r.at[k * count_z + g])
                part[band(g), c] = part[band(g), c] + next_x[band(g), c]

        result_sends(k, begin)

    def step(k, carry):
        @pl.when(k < count_y)
        def _():
            project(k)

        @pl.when(k > 0)
        def _():
            diverge(k - 1)
        return carry

    lax.fori_loop(0, count_y + 1, step, 0)

    def collect(i, carry):
        y = wrap(py - i - 1)
        for z in range(count_z):
            q = y * count_z + z
            landed(got.at[q], a_r.at[q])
            added = jnp.minimum(planes - 1 - q, 1 - passed_up(z, pz))

            @pl.when(added > 0)
            def _():
                landed(got_x.at[q], x_r.at[q])
                div[q] = got[q] + got_x[q]

            @pl.when(added <= 0)
            def _():
                div[q] = got[q]
        return carry

    lax.fori_loop(0, count_y, collect, 0)

    def finish(k, carry):
        pressure_sends(k, sent)
        fluid_sends(k, sent)
        forward(k, sent)
        lend(k, sent)
        result_sends(k, sent)
        return carry

    edge_sends(sent)
    lax.fori_loop(0, count_y, finish, 0)


def on_device(velocity, fluid, pressure):
    count_y = lax.axis_size("py")
    count_z = lax.axis_size("pz")
    rows, across = fluid.shape[1:]
    planes = pressure.shape[0]
    block = pressure.shape[1:]
    vm = lambda *shape: pltpu.VMEM(shape, jnp.float32)
    dma = lambda n: pltpu.SemaphoreType.DMA((n,))
    steps = count_y * count_z
    return pl.pallas_call(
        functools.partial(kernel, count_y, count_z),
        out_shape=(
            jax.ShapeDtypeStruct(velocity.shape, jnp.float32),
            jax.ShapeDtypeStruct(pressure.shape, jnp.float32),
        ),
        in_specs=[pl.BlockSpec(memory_space=pltpu.MemorySpace.HBM)] * 3,
        out_specs=(pl.BlockSpec(memory_space=pltpu.VMEM),) * 2,
        scratch_shapes=[
            vm(3, rows, across), vm(rows, across), vm(rows, across), vm(rows, across), vm(rows, across),
            vm(rows, LANES), vm(rows, across), vm(rows, across),
            vm(planes, *block), vm(planes, *block), dma(2),
            dma(steps), dma(steps), dma(steps), dma(steps), dma(count_z), dma(count_z),
            dma(count_y), dma(count_y), dma(steps), dma(steps), dma(steps), dma(steps),
            dma(steps), dma(planes), dma(steps), dma(planes),
        ],
        compiler_params=pltpu.CompilerParams(
            collective_id=0, has_side_effects=True, vmem_limit_bytes=40 << 20
        ),
        name="project_all",
    )(*(pltpu.with_memory_space_constraint(x, pltpu.MemorySpace.HBM) for x in (velocity, fluid, pressure)))


def solution(mesh):
    placed = (P(None, ("py", "pz"), None, None), P(("py", "pz"), None, None), P(None, "pz", "py"))
    return jax.shard_map(
        on_device,
        mesh=mesh,
        in_specs=placed,
        out_specs=(P(None, ("py", "pz"), None, None), P(None, "pz", "py")),
        check_vma=False,
    )
```
